32 devices in a mesh: groups: 2 (over x), face: 8 (over z, y), sub: 2 (over core).
Axes of the slice: x: 2, y: 2, z: 4, core: 2. Of those that a mesh axis runs over, the one named last changes fastest.
Arguments:
- features: bfloat16 [65536, 64], P(('groups', 'face', 'sub')), parts along dimension 0
- links_fine: int32 [9, 32768], P(None, ('face', 'sub')), may hold values from 0 to 2175, as said below
- sends_fine: int32 [16, 2, 64], P(('face', 'sub')), may hold values from 0 to 2047, as said below
- links_mid: int32 [9, 8192], P(None, ('face', 'sub')), may hold values from 0 to 575, as said below
- sends_mid: int32 [16, 2, 32], P(('face', 'sub')), may hold values from 0 to 511, as said below
- links_coarse: int32 [9, 2048], P(None, ('face', 'sub')), may hold values from 0 to 159, as said below
- sends_coarse: int32 [16, 2, 16], P(('face', 'sub')), may hold values from 0 to 127, as said below
- kernel_enter: bfloat16 [9, 64, 128], replicated, may hold values from -0.25 to 0.25
- gain_enter: float32 [128], replicated, may hold values from 0.5 to 1.5
- shift_enter: float32 [128], replicated, may hold values from -2.5 to 2.5
- kernel_fine: bfloat16 [9, 128, 128], replicated, may hold values from -0.1875 to 0.1875
- gain_fine: float32 [128], replicated, may hold values from 0.5 to 1.5
- shift_fine: float32 [128], replicated, may hold values from -2.5 to 2.5
- kernel_widen: bfloat16 [9, 128, 256], replicated, may hold values from -0.1875 to 0.1875
- gain_widen: float32 [256], replicated, may hold values from 0.5 to 1.5
- shift_widen: float32 [256], replicated, may hold values from -2.5 to 2.5
- kernel_mid: bfloat16 [9, 256, 256], replicated, may hold values from -0.125 to 0.125
- gain_mid: float32 [256], replicated, may hold values from 0.5 to 1.5
- shift_mid: float32 [256], replicated, may hold values from -2.5 to 2.5
- kernel_deep: bfloat16 [9, 256, 512], replicated, may hold values from -0.125 to 0.125
- gain_deep: float32 [512], replicated, may hold values from 0.5 to 1.5
- shift_deep: float32 [512], replicated, may hold values from -2.5 to 2.5
Outputs:
- skip_fine: bfloat16 [65536, 128], P(('groups', 'face', 'sub')), parts along dimension 0
- skip_mid: bfloat16 [16384, 256], P(('groups', 'face', 'sub')), parts along dimension 0
- bottleneck: bfloat16 [4096, 512], P(('groups', 'face', 'sub')), parts along dimension 0
The draws below stay inside these ranges and needn't reach their ends.
There are 2 independent parts, one for each index of `groups`. The reference program is written for one: setup_inputs(seed, part) draws one part's arguments, and reference() takes and returns one part's arrays. A program takes and returns all parts, laid end to end along the dimension named above; an argument that names none is the same for every part. Nothing has to cross between parts.
Inputs may be any that keep to these rules, and one draw needn't show every extreme that they name: links_fine[0, p] is p's own row within its range; every entry below 2048 is a row of the own range, entries from 2048 on index the padded block's received rows. sends_fine[g, 0] lists range g's first 64 rows in some order, sends_fine[g, 1] its last 64 rows in some order. links_mid[0, p] is p's own row within its range; entries from 512 on index the padded block's received rows. sends_mid[g, 0] lists range g's first 32 rows in some order, sends_mid[g, 1] its last 32 rows in some order. links_coarse[0, p] is p's own row within its range; entries from 128 on index the padded block's received rows. sends_coarse[g, 0] lists range g's first 16 rows in some order, sends_coarse[g, 1] its last 16 rows in some order.
All inputs are finite; a program needn't handle non-finite values.
Results may differ from the reference program's by a relative error of at most 0.011.
Values may be sent and summed in bfloat16 or wider, within the bound.
No kernel may reach another device: no remote copies, remote signals or barrier semaphores. Data moves between devices by JAX's collectives and lax.ppermute only.
A program may use at most 64 MiB of HBM per device.

```python
import jax
import jax.numpy as jnp
from jax import lax

C_IN = 64
C_A = 128
C_B = 256
C_C = 512
ROWS_DEV = 2048
RANGES = 16
ROWS_B = 512
ROWS_C = 128
HALO_A = 64
HALO_B = 32
HALO_C = 16
PIX_A = 32768


def neighbour_table(key, rows, halo):
    offsets = jax.random.randint(key, (RANGES, rows, 8), -halo, halo + 1)
    offsets = offsets.at[:, rows - 1, 7].set(halo)
    own = jnp.arange(rows, dtype=jnp.int32)[None, :, None]
    target = own + offsets
    local = jnp.where(target < 0, target + rows + halo, jnp.where(target >= rows, target + halo, target))
    centre = jnp.broadcast_to(own, (RANGES, rows, 1))
    table = jnp.concatenate([centre, local], axis=2).reshape(RANGES * rows, 9)
    return jnp.transpose(table).astype(jnp.int32)


def send_lists(key, rows, halo):
    keys = jax.random.split(key, 2 * RANGES)
    orders = jax.vmap(lambda single: jax.random.permutation(single, halo))(keys).reshape(RANGES, 2, halo)
    first = orders[:, 0, :]
    last = rows - 1 - orders[:, 1, :]
    return jnp.stack([first, last], axis=1).astype(jnp.int32)


def draw_features(key, part):
    key_base, key_row, key_col = jax.random.split(jax.random.fold_in(key, 7), 3)
    rows = jnp.arange(PIX_A).astype(jnp.float32)
    rising = jnp.exp(jnp.log(3.0) * rows / PIX_A)[:, None]
    base = jax.random.normal(key_base, (PIX_A, C_IN), jnp.float32)
    row_scale = jnp.exp(jax.random.uniform(key_row, (PIX_A, 1), jnp.float32, 0.0, jnp.log(10.0)))
    col_scale = jnp.exp(jax.random.uniform(key_col, (1, C_IN), jnp.float32, 0.0, jnp.log(10.0)))
    return (base * rising * row_scale * col_scale / 12.0).astype(jnp.bfloat16)


def draw_links_fine(key, part):
    return neighbour_table(jax.random.fold_in(key, 11), ROWS_DEV, HALO_A)


def draw_links_mid(key, part):
    return neighbour_table(jax.random.fold_in(key, 12), ROWS_B, HALO_B)


def draw_links_coarse(key, part):
    return neighbour_table(jax.random.fold_in(key, 13), ROWS_C, HALO_C)


def draw_sends_fine(key, part):
    return send_lists(jax.random.fold_in(key, 21), ROWS_DEV, HALO_A)


def draw_sends_mid(key, part):
    return send_lists(jax.random.fold_in(key, 22), ROWS_B, HALO_B)


def draw_sends_coarse(key, part):
    return send_lists(jax.random.fold_in(key, 23), ROWS_C, HALO_C)


def normal_values(stream_key, dims, deviation, most, kind=jnp.bfloat16):
    return jnp.clip(deviation * jax.random.normal(stream_key, dims, jnp.float32), -most, most).astype(kind)


def setup_inputs(seed: int = 0, part: int = 0) -> dict:
    key_of = jax.random.split(jax.random.key(seed), 23)
    part_splits = jax.random.split(jax.random.fold_in(key_of[22], part), 23)
    features = draw_features(jax.random.fold_in(jax.random.fold_in(key_of[22], part), 71), part)
    links_fine = draw_links_fine(jax.random.fold_in(key_of[22], 71), part)
    sends_fine = draw_sends_fine(jax.random.fold_in(key_of[22], 71), part)
    links_mid = draw_links_mid(jax.random.fold_in(key_of[22], 71), part)
    sends_mid = draw_sends_mid(jax.random.fold_in(key_of[22], 71), part)
    links_coarse = draw_links_coarse(jax.random.fold_in(key_of[22], 71), part)
    sends_coarse = draw_sends_coarse(jax.random.fold_in(key_of[22], 71), part)
    kernel_enter = normal_values(key_of[7], (9, C_IN, C_A), (9 * C_IN) ** -0.5, 0.25)
    gain_enter = jnp.clip(1.0 + 0.1 * jax.random.normal(key_of[8], (C_A,), jnp.float32), 0.5, 1.5)
    shift_enter = normal_values(key_of[9], (C_A,), 0.5, 2.5, jnp.float32)
    kernel_fine = normal_values(key_of[10], (9, C_A, C_A), (9 * C_A) ** -0.5, 0.1875)
    gain_fine = jnp.clip(1.0 + 0.1 * jax.random.normal(key_of[11], (C_A,), jnp.float32), 0.5, 1.5)
    shift_fine = normal_values(key_of[12], (C_A,), 0.5, 2.5, jnp.float32)
    kernel_widen = normal_values(key_of[13], (9, C_A, C_B), (9 * C_A) ** -0.5, 0.1875)
    gain_widen = jnp.clip(1.0 + 0.1 * jax.random.normal(key_of[14], (C_B,), jnp.float32), 0.5, 1.5)
    shift_widen = normal_values(key_of[15], (C_B,), 0.5, 2.5, jnp.float32)
    kernel_mid = normal_values(key_of[16], (9, C_B, C_B), (9 * C_B) ** -0.5, 0.125)
    gain_mid = jnp.clip(1.0 + 0.1 * jax.random.normal(key_of[17], (C_B,), jnp.float32), 0.5, 1.5)
    shift_mid = normal_values(key_of[18], (C_B,), 0.5, 2.5, jnp.float32)
    kernel_deep = normal_values(key_of[19], (9, C_B, C_C), (9 * C_B) ** -0.5, 0.125)
    gain_deep = jnp.clip(1.0 + 0.1 * jax.random.normal(key_of[20], (C_C,), jnp.float32), 0.5, 1.5)
    shift_deep = normal_values(key_of[21], (C_C,), 0.5, 2.5, jnp.float32)
    return dict(features=features, links_fine=links_fine, sends_fine=sends_fine, links_mid=links_mid, sends_mid=sends_mid, links_coarse=links_coarse, sends_coarse=sends_coarse, kernel_enter=kernel_enter, gain_enter=gain_enter, shift_enter=shift_enter, kernel_fine=kernel_fine, gain_fine=gain_fine, shift_fine=shift_fine, kernel_widen=kernel_widen, gain_widen=gain_widen, shift_widen=shift_widen, kernel_mid=kernel_mid, gain_mid=gain_mid, shift_mid=shift_mid, kernel_deep=kernel_deep, gain_deep=gain_deep, shift_deep=shift_deep)


def level_conv(feat, sends, links, kernel):
    ranges = sends.shape[0]
    rows = feat.shape[0] // ranges
    blocks = feat.reshape(ranges, rows, feat.shape[1])
    to_left = jnp.take_along_axis(blocks, sends[:, 0, :, None], axis=1)
    to_right = jnp.take_along_axis(blocks, sends[:, 1, :, None], axis=1)
    padded = jnp.concatenate([blocks, jnp.roll(to_right, 1, axis=0), jnp.roll(to_left, -1, axis=0)], axis=1)
    index = links.reshape(9, ranges, rows)
    total = jnp.zeros((feat.shape[0], kernel.shape[2]), jnp.float32)
    for tap in range(9):
        picked = jnp.take_along_axis(padded, index[tap][:, :, None], axis=1)
        total = total + jnp.dot(picked.reshape(feat.shape[0], feat.shape[1]), kernel[tap], preferred_element_type=jnp.float32)
    return total

def activate(total, gain, shift):
    mean = lax.optimization_barrier(jnp.mean(total, axis=0))
    centered = total - mean
    var = lax.optimization_barrier(jnp.mean(centered * centered, axis=0))
    normed = centered * lax.rsqrt(var + 1e-05) * gain + shift
    return jax.nn.gelu(normed, approximate=False).astype(jnp.bfloat16)

def pooling(act):
    return lax.optimization_barrier(jnp.mean(act.reshape(-1, 4, act.shape[1]).astype(jnp.float32), axis=1)).astype(jnp.bfloat16)

def reference(features, links_fine, sends_fine, links_mid, sends_mid, links_coarse, sends_coarse, kernel_enter, gain_enter, shift_enter, kernel_fine, gain_fine, shift_fine, kernel_widen, gain_widen, shift_widen, kernel_mid, gain_mid, shift_mid, kernel_deep, gain_deep, shift_deep):
    first_fine = activate(level_conv(features, sends_fine, links_fine, kernel_enter), gain_enter, shift_enter)
    skip_fine = activate(level_conv(first_fine, sends_fine, links_fine, kernel_fine), gain_fine, shift_fine)
    pooled_mid = pooling(skip_fine)
    first_mid = activate(level_conv(pooled_mid, sends_mid, links_mid, kernel_widen), gain_widen, shift_widen)
    skip_mid = activate(level_conv(first_mid, sends_mid, links_mid, kernel_mid), gain_mid, shift_mid)
    pooled_coarse = pooling(skip_mid)
    bottleneck = activate(level_conv(pooled_coarse, sends_coarse, links_coarse, kernel_deep), gain_deep, shift_deep)
    return (skip_fine, skip_mid, bottleneck)
```

```python
import functools

import jax
import jax.numpy as jnp
from jax import lax
from jax.experimental import pallas as pl
from jax.experimental.pallas import tpu as pltpu
from jax.sharding import PartitionSpec as P

AXES = ("face", "sub")
BLOCK = 128
WINDOW = 256
TAPS = 9
EPS = 1e-05
VM = pl.BlockSpec(memory_space=pltpu.VMEM)
SM = pl.BlockSpec(memory_space=pltpu.SMEM)


def shifted(value, steps):
    count = lax.axis_size(AXES)
    return lax.ppermute(value, AXES, [(source, (source + steps) % count) for source in range(count)])


def picker(column, width, offset=0):
    places = lax.broadcasted_iota(jnp.int32, (column.shape[0], width), 1) + offset
    return jnp.where(column == places, 1.0, 0.0).astype(jnp.bfloat16)


def listed(rows, order, start):
    halo = rows.shape[0]
    column = jnp.transpose(jnp.broadcast_to(order, (BLOCK, BLOCK)))[start : start + halo, :halo]
    places = lax.broadcasted_iota(jnp.int32, (halo, halo), 1).astype(jnp.float32)
    chosen = jnp.where(column == places, 1.0, 0.0).astype(jnp.bfloat16)
    return jnp.dot(chosen, rows, preferred_element_type=jnp.float32).astype(jnp.bfloat16)


def gathered(sources, column_of, start, width):
    parts = []
    if len(sources) == 1:
        window = sources[0][pl.ds(start, width), :]
        for tap in range(1, TAPS):
            hot = picker(column_of(tap), width)
            parts.append(jnp.dot(hot, window, preferred_element_type=jnp.float32).astype(jnp.bfloat16))
        return parts
    low = sources[0][pl.ds(start, width), :]
    high = sources[1][pl.ds(start, width), :]
    parts.append(jnp.dot(picker(column_of(1), width), high, preferred_element_type=jnp.float32))
    for tap in range(2, TAPS, 2):
        pair = jnp.dot(picker(column_of(tap), width), low, preferred_element_type=jnp.float32)
        if tap + 1 < TAPS:
            pair = pair + jnp.dot(picker(column_of(tap + 1), width), high, preferred_element_type=jnp.float32)
        parts.append(pair)
    return [part.astype(jnp.bfloat16) for part in parts]


def convolve(sources, links, spans, weights, total, halo):
    rows, depth = total.shape[0], weights.shape[0]
    padded = sources[0].shape[0]
    paired = len(sources) == 2

    def joined(parts, own):
        if paired:
            parts = [parts[0] + own] + parts[1:]
        else:
            parts = [own] + parts
        return jnp.concatenate(parts, axis=1)[:, :depth]

    def main(block, carry):
        start = pl.multiple_of(block * BLOCK, BLOCK)
        near = links[pl.ds(start, BLOCK), :] - start
        parts = gathered(sources, lambda tap: near[:, tap - 1 : tap], start, WINDOW)
        own = sources[0][pl.ds(pl.multiple_of(start + halo, 16), BLOCK), :]
        total[pl.ds(start, BLOCK), :] = jnp.dot(joined(parts, own), weights[...], preferred_element_type=jnp.float32)
        return carry

    lax.fori_loop(0, rows // BLOCK, main, 0)
    if padded <= WINDOW:
        return

    @pl.when(spans[2, 0] > 0)
    def _():
        def rest(block, carry):
            start = pl.multiple_of(block * BLOCK, BLOCK)

            def chunk(place, inner):
                @pl.when((place < block) | (place > block + 1))
                def _():
                    first = pl.multiple_of(place * BLOCK, BLOCK)
                    near = links[pl.ds(start, BLOCK), :] - first
                    parts = gathered(sources, lambda tap: near[:, tap - 1 : tap], first, BLOCK)
                    own = jnp.zeros((BLOCK, sources[0].shape[1]), jnp.bfloat16)
                    total[pl.ds(start, BLOCK), :] += jnp.dot(
                        joined(parts, own), weights[...], preferred_element_type=jnp.float32
                    )

                return inner

            return lax.fori_loop(spans[0, block], spans[1, block] + 1, chunk, carry)

        lax.fori_loop(0, rows // BLOCK, rest, 0)


def summarize(total, to_next, to_last, stats):
    rows, channels = total.shape
    edge = to_next.shape[0] - 8
    pieces = 8
    size = rows // pieces
    sums = [jnp.sum(total[i * size : (i + 1) * size, :], axis=0, keepdims=True) for i in range(pieces)]
    mean = functools.reduce(jnp.add, sums) / rows
    squares = []
    for i in range(pieces):
        centred = total[i * size : (i + 1) * size, :] - mean
        squares.append(jnp.sum(centred * centred, axis=0, keepdims=True))
    pair = jnp.concatenate([mean, functools.reduce(jnp.add, squares)], axis=0)
    stats[...] = pair
    if edge > 0:
        tail = jnp.concatenate([pair, jnp.zeros((6, channels), jnp.float32)], axis=0)
        to_next[edge:, :] = tail
        to_last[edge:, :] = tail
        to_next[:edge, :] = total[rows - edge :, :]
        to_last[:edge, :] = total[:edge, :]


def enter_kernel(halo, feat, left, right, order, links, spans, weights, total, to_next, to_last, stats, low, high):
    rows, width = feat.shape
    blank = jnp.zeros((rows, width), jnp.bfloat16)
    edge = jnp.zeros((halo, width), jnp.bfloat16)
    before = listed(left[:halo, :], order[0:1, :], 0)
    after = listed(right[:halo, :], order[1:2, :], 0)
    low[halo : halo + rows, :] = jnp.concatenate([feat[...], blank], axis=1)
    high[halo : halo + rows, :] = jnp.concatenate([blank, feat[...]], axis=1)
    low[:halo, :] = jnp.concatenate([before, edge], axis=1)
    high[:halo, :] = jnp.concatenate([edge, before], axis=1)
    low[halo + rows :, :] = jnp.concatenate([after, edge], axis=1)
    high[halo + rows :, :] = jnp.concatenate([edge, after], axis=1)
    convolve((low, high), links, spans, weights, total, halo)
    summarize(total, to_next, to_last, stats)


def combined(pairs, count):
    mean = functools.reduce(jnp.add, [pair[0:1, :] for pair in pairs]) / len(pairs)
    spread = functools.reduce(jnp.add, [(pair[0:1, :] - mean) * (pair[0:1, :] - mean) for pair in pairs])
    squares = functools.reduce(jnp.add, [pair[1:2, :] for pair in pairs]) + count * spread
    return mean, squares


def norm_of(pairs, count, gain, shift):
    mean, squares = combined([pair[...] for pair in pairs], count)
    scale = lax.rsqrt(squares / (count * len(pairs)) + EPS) * gain[...]
    offset = shift[...]

    def act(raw):
        normed = (raw - mean) * scale + offset
        return (normed * (1.0 + lax.erf(normed * 0.7071067811865476)) * 0.5).astype(jnp.bfloat16)

    return act


def pooled(act):
    rows = act.shape[0]
    row = lax.broadcasted_iota(jnp.int32, (rows // 4, rows), 0)
    col = lax.broadcasted_iota(jnp.int32, (rows // 4, rows), 1)
    quarter = jnp.where((col >= 4 * row) & (col < 4 * row + 4), 0.25, 0.0).astype(jnp.bfloat16)
    return jnp.dot(quarter, act, preferred_element_type=jnp.float32).astype(jnp.bfloat16)


def layer_kernel(halo, listing, pool, count, parts, *refs):
    raw, left, right, order, gain, shift, links, spans, weights = refs[:9]
    pairs = refs[9 : 9 + parts]
    outs = refs[9 + parts :]
    if pool:
        skip, outs = outs[0], outs[1:]
    total, to_next, to_last, stats, source = outs
    act = norm_of(pairs, count, gain, shift)
    rows = total.shape[0]
    fold = pooled if pool else (lambda value: value)
    reach = halo * 4 if pool else halo
    source[:halo, :] = listed(fold(act(left[:reach, :])), order[0:1, :], listing)
    source[halo + rows : rows + 2 * halo, :] = listed(fold(act(right[:reach, :])), order[1:2, :], listing)
    if source.shape[0] > rows + 2 * halo:
        source[rows + 2 * halo :, :] = jnp.zeros((source.shape[0] - rows - 2 * halo, source.shape[1]), jnp.bfloat16)
    step = BLOCK
    out_step = step // 4 if pool else step

    def one(i, carry):
        start = pl.multiple_of(i * step, step)
        value = act(raw[pl.ds(start, step), :])
        if pool:
            skip[pl.ds(start, step), :] = value
        source[pl.ds(pl.multiple_of(i * out_step + halo, 16), out_step), :] = fold(value)
        return carry

    lax.fori_loop(0, raw.shape[0] // step, one, 0)
    convolve((source,), links, spans, weights, total, halo)
    summarize(total, to_next, to_last, stats)


def last_kernel(count, parts, *refs):
    raw, gain, shift = refs[:3]
    out = refs[3 + parts]
    out[...] = norm_of(refs[3 : 3 + parts], count, gain, shift)(raw[...])


def call(body, outs, scratch, *args, smem=(), name):
    return pl.pallas_call(
        body,
        out_shape=outs,
        in_specs=[SM if i in smem else VM for i in range(len(args))],
        out_specs=[VM] * len(outs) if isinstance(outs, (list, tuple)) else VM,
        scratch_shapes=scratch,
        compiler_params=pltpu.CompilerParams(vmem_limit_bytes=32 * 1024 * 1024),
        name=name,
    )(*args)


def table(links, rows, halo):
    places = jnp.where(links < rows, links + halo, jnp.where(links < rows + halo, links - rows, links))[1:]
    by_block = places.reshape(TAPS - 1, rows // BLOCK, BLOCK)
    first = jnp.min(by_block, axis=(0, 2)) // BLOCK
    final = jnp.max(by_block, axis=(0, 2)) // BLOCK
    block = jnp.arange(rows // BLOCK)
    outside = jnp.any((first < block) | (final > block + 1)).astype(jnp.int32)
    spans = jnp.stack([first, final, jnp.full_like(first, outside)])
    return jnp.transpose(places), spans


def phases(count):
    steps, stride, left = [], 4, count // 4
    while left > 1:
        radix = 4 if left % 4 == 0 else (2 if left % 2 == 0 else left)
        steps.append([stride * i for i in range(1, radix)])
        stride, left = stride * radix, left // radix
    return steps


def gather_stats(pairs, rows, count):
    held = rows
    for steps in phases(count):
        mean, squares = combined(pairs, held)
        held = held * len(pairs)
        mine = jnp.concatenate([mean, squares], axis=0)
        pairs = [mine] + [shifted(mine, step) for step in steps]
    return pairs, held


def exchange(to_next, to_last, stats, rows, edge):
    count = lax.axis_size(AXES)
    from_left = shifted(to_next, 1)
    from_right = shifted(to_last, -1)
    across = shifted(stats, 2)
    pairs = [stats, from_left[edge : edge + 2], from_right[edge : edge + 2], across]
    pairs, held = gather_stats(pairs, rows, count)
    return from_left, from_right, pairs, held


def stats_only(stats, rows):
    count = lax.axis_size(AXES)
    pairs = [stats, shifted(stats, 1), shifted(stats, -1), shifted(stats, 2)]
    return gather_stats(pairs, rows, count)


def f32(*shape):
    return jax.ShapeDtypeStruct(shape, jnp.float32)


def bf16(*shape):
    return jax.ShapeDtypeStruct(shape, jnp.bfloat16)


def conv_outs(rows, channels, edge):
    return [f32(rows, channels), f32(edge + 8, channels), f32(edge + 8, channels), f32(2, channels)]


def round_up(value, unit):
    return -(-value // unit) * unit


def per_device(
    features,
    links_fine,
    sends_fine,
    links_mid,
    sends_mid,
    links_coarse,
    sends_coarse,
    kernel_enter,
    gain_enter,
    shift_enter,
    kernel_fine,
    gain_fine,
    shift_fine,
    kernel_widen,
    gain_widen,
    shift_widen,
    kernel_mid,
    gain_mid,
    shift_mid,
    kernel_deep,
    gain_deep,
    shift_deep,
):
    rows_a, rows_b, rows_c = links_fine.shape[1], links_mid.shape[1], links_coarse.shape[1]
    halo_a, halo_b, halo_c = sends_fine.shape[2], sends_mid.shape[2], sends_coarse.shape[2]
    width = features.shape[1]
    weights = [
        kernel.reshape(TAPS * kernel.shape[1], kernel.shape[2])
        for kernel in (kernel_enter, kernel_fine, kernel_widen, kernel_mid, kernel_deep)
    ]
    c_a, c_b, c_c = kernel_enter.shape[2], kernel_widen.shape[2], kernel_deep.shape[2]

    def packed(rows, lists):
        flat = jnp.concatenate(lists).astype(jnp.bfloat16)
        flat = jnp.pad(flat, (0, BLOCK - flat.shape[0])).reshape(-1, width)
        return jnp.concatenate([rows, jnp.pad(flat, ((0, 16 - flat.shape[0]), (0, 0)))], axis=0)

    last_lists = [
        sends_fine[0, 1] - (rows_a - halo_a),
        sends_mid[0, 1] - (rows_b - halo_b),
        sends_coarse[0, 1] - (rows_c - halo_c),
    ]
    first_lists = [sends_fine[0, 0], sends_mid[0, 0], sends_coarse[0, 0]]
    left = shifted(packed(features[rows_a - halo_a :], last_lists), 1)
    right = shifted(packed(features[:halo_a], first_lists), -1)
    words = BLOCK // width
    order = jnp.concatenate(
        [side[halo_a : halo_a + words].reshape(1, BLOCK).astype(jnp.float32) for side in (left, right)], axis=0
    )

    places_a, spans_a = table(links_fine, rows_a, halo_a)
    places_b, spans_b = table(links_mid, rows_b, halo_b)
    places_c, spans_c = table(links_coarse, rows_c, halo_c)

    source_a = pltpu.VMEM((round_up(rows_a + 2 * halo_a, BLOCK), 2 * width), jnp.bfloat16)
    total, to_next, to_last, stats = call(
        functools.partial(enter_kernel, halo_a),
        conv_outs(rows_a, c_a, halo_a),
        [source_a, source_a],
        features,
        left,
        right,
        order,
        places_a,
        spans_a,
        weights[0],
        smem=(5,),
        name="enter",
    )

    def layer(total, to_next, to_last, stats, edge, gain, shift, level, kernel, pool, out_edge, name):
        rows, halo, listing, places, spans = level
        raw_rows, channels = total.shape
        from_left, from_right, pairs, held = exchange(to_next, to_last, stats, raw_rows, edge)
        outs = conv_outs(rows, kernel.shape[1], out_edge)
        if pool:
            outs = [bf16(raw_rows, channels)] + outs
        return call(
            functools.partial(layer_kernel, halo, listing, pool, held, len(pairs)),
            outs,
            [pltpu.VMEM((max(round_up(rows + 2 * halo, BLOCK), WINDOW), channels), jnp.bfloat16)],
            total,
            from_left,
            from_right,
            order,
            gain.reshape(1, -1),
            shift.reshape(1, -1),
            places,
            spans,
            kernel,
            *pairs,
            smem=(7,),
            name=name,
        )

    level_a = (rows_a, halo_a, 0, places_a, spans_a)
    level_b = (rows_b, halo_b, halo_a, places_b, spans_b)
    level_c = (rows_c, halo_c, halo_a + halo_b, places_c, spans_c)
    state = (total, to_next, to_last, stats)
    state = layer(*state, halo_a, gain_enter, shift_enter, level_a, weights[1], False, 4 * halo_b, "fine")
    skip_fine, *state = layer(*state, 4 * halo_b, gain_fine, shift_fine, level_b, weights[2], True, halo_b, "widen")
    state = layer(*state, halo_b, gain_widen, shift_widen, level_b, weights[3], False, 4 * halo_c, "mid")
    skip_mid, *state = layer(*state, 4 * halo_c, gain_mid, shift_mid, level_c, weights[4], True, 8, "deep")
    total, _, _, stats = state
    pairs, held = stats_only(stats, rows_c)
    bottleneck = call(
        functools.partial(last_kernel, held, len(pairs)),
        bf16(rows_c, c_c),
        [],
        total,
        gain_deep.reshape(1, -1),
        shift_deep.reshape(1, -1),
        *pairs,
        name="last",
    )
    return (skip_fine, skip_mid, bottleneck)


def solution(mesh):
    split = P(("groups", "face", "sub"), None)
    links, sends = P(None, AXES), P(AXES, None, None)
    return jax.shard_map(
        per_device,
        mesh=mesh,
        in_specs=(split, links, sends, links, sends, links, sends) + (P(),) * 15,
        out_specs=(split, split, split),
        check_vma=False,
    )
```

```python
import functools

import jax
import jax.numpy as jnp
from jax import lax
from jax.experimental import pallas as pl
from jax.experimental.pallas import tpu as pltpu
from jax.sharding import PartitionSpec as P


AXES = ("face", "sub")
BLOCK = 128
WINDOW = 256
TAPS = 9
EPS = 1e-05
VM = pl.BlockSpec(memory_space=pltpu.VMEM)
HERE = pl.BlockSpec(memory_space=pltpu.HBM)


def shifted(value, steps):
    count = lax.axis_size(AXES)
    return lax.ppermute(value, AXES, [(source, (source + steps) % count) for source in range(count)])


def swapped(value, mask):
    count = lax.axis_size(AXES)
    return lax.ppermute(value, AXES, [(source, source ^ mask) for source in range(count)])


def hots(near, width):
    places = lax.broadcasted_iota(jnp.int32, (near.shape[0], width), 1)
    return [jnp.where(near[:, tap : tap + 1] == places, 1.0, 0.0).astype(jnp.bfloat16) for tap in range(TAPS - 1)]


def listed(rows, order, start):
    halo = rows.shape[0]
    column = jnp.transpose(jnp.broadcast_to(order, (BLOCK, BLOCK)))[start : start + halo, :halo]
    places = lax.broadcasted_iota(jnp.int32, (halo, halo), 1).astype(jnp.float32)
    chosen = jnp.where(column == places, 1.0, 0.0).astype(jnp.bfloat16)
    return jnp.dot(chosen, rows, preferred_element_type=jnp.float32).astype(jnp.bfloat16)


def dot(a, b):
    return jnp.dot(a, b, preferred_element_type=jnp.float32)


def picked(sources, near, start, width):
    hot = hots(near, width)
    if len(sources) == 1:
        window = sources[0][pl.ds(start, width), :]
        rows = dot(jnp.concatenate(hot, axis=0), window).astype(jnp.bfloat16)
        return [rows[i * BLOCK : (i + 1) * BLOCK] for i in range(TAPS - 1)]
    low = dot(jnp.concatenate(hot[1::2], axis=0), sources[0][pl.ds(start, width), :])
    high = dot(jnp.concatenate(hot[0::2], axis=0), sources[1][pl.ds(start, width), :])
    low = [low[i * BLOCK : (i + 1) * BLOCK] for i in range(4)]
    high = [high[i * BLOCK : (i + 1) * BLOCK] for i in range(4)]
    pieces = [high[0]] + [low[i] + high[i + 1] for i in range(3)] + [low[3]]
    return [piece.astype(jnp.bfloat16) for piece in pieces]


def convolve(sources, links, weights, total, columns, halo):
    rows, depth = total.shape[0], weights.shape[0]
    padded, lanes = sources[0].shape
    paired = len(sources) == 2

    def places(block):
        link = links[1:, pl.ds(pl.multiple_of(block * BLOCK, BLOCK), BLOCK)]
        place = jnp.where(link < rows, link + halo, jnp.where(link < rows + halo, link - rows, link))
        return jnp.transpose(place)

    def main(block, far):
        start = pl.multiple_of(block * BLOCK, BLOCK)
        near = places(block) - start
        own = sources[0][pl.ds(pl.multiple_of(start + halo, 16), BLOCK), :]
        pieces = picked(sources, near, start, WINDOW)
        pieces = [pieces[0] + own] + pieces[1:] if paired else [own] + pieces
        for i, piece in enumerate(pieces):
            columns[pl.ds(start, BLOCK), i * lanes : (i + 1) * lanes] = piece
        return jnp.maximum(far, jnp.where((near < 0) | (near >= WINDOW), 1, 0))

    far = lax.fori_loop(0, rows // BLOCK, main, jnp.zeros((BLOCK, TAPS - 1), jnp.int32), unroll=min(2, rows // BLOCK))
    step = min(rows, 512)

    def multiply(i, carry):
        part = pl.ds(pl.multiple_of(i * step, step), step)
        total[part, :] = dot(columns[part, :depth], weights[...])
        return carry

    lax.fori_loop(0, rows // step, multiply, 0)
    if padded <= WINDOW:
        return

    @pl.when(jnp.max(far) > 0)
    def _():
        def rest(block, carry):
            start = pl.multiple_of(block * BLOCK, BLOCK)

            def chunk(place, inner):
                @pl.when((place < block) | (place > block + 1))
                def _():
                    first = pl.multiple_of(place * BLOCK, BLOCK)
                    pieces = picked(sources, places(block) - first, first, BLOCK)
                    pieces = pieces if paired else [jnp.zeros_like(pieces[0])] + pieces
                    gathered = jnp.concatenate(pieces, axis=1)[:, :depth]
                    total[pl.ds(start, BLOCK), :] += dot(gathered, weights[...])

                return inner

            return lax.fori_loop(0, padded // BLOCK, chunk, carry)

        lax.fori_loop(0, rows // BLOCK, rest, 0)


def summarize(total, stats, *edges):
    rows, _ = total.shape
    pieces = 8
    size = rows // pieces
    sums = [jnp.sum(total[i * size : (i + 1) * size, :], axis=0, keepdims=True) for i in range(pieces)]
    mean = functools.reduce(jnp.add, sums) / rows
    squares = []
    for i in range(pieces):
        centred = total[i * size : (i + 1) * size, :] - mean
        squares.append(jnp.sum(centred * centred, axis=0, keepdims=True))
    stats[...] = jnp.concatenate([mean, functools.reduce(jnp.add, squares)], axis=0)
    for target, start in zip(edges, (0, rows)):
        edge = target.shape[0]
        target[...] = total[start - edge if start else 0 : start or edge, :]


def start_copies(pairs, sems):
    copies = [pltpu.make_async_copy(source, target, sems.at[i]) for i, (source, target) in enumerate(pairs)]
    for copy in copies:
        copy.start()
    return copies


def pack_kernel(inner, feat, sends_a, sends_b, sends_c, to_last, to_next, first, final, *scratch):
    held, sems = scratch[:3], scratch[3]
    width, rows = feat.shape
    pairs = [(feat.at[:, :BLOCK], first), (feat.at[:, rows - BLOCK :], final)]
    for copy in start_copies(pairs + list(zip((sends_a, sends_b, sends_c), held)), sems):
        copy.wait()
    halo = to_next.shape[0] - 16
    for target, edge, side in ((to_last, first, 0), (to_next, final, 1)):
        turned = jnp.transpose(edge[...].astype(jnp.float32))
        turned = turned[BLOCK - halo :] if side else turned[:halo]
        lists = [sends[0, side : side + 1, :] - before * side for sends, before in zip(held, inner)]
        used = sum(part.shape[1] for part in lists)
        order = jnp.concatenate(lists + [jnp.zeros((1, BLOCK - used), jnp.int32)], axis=1).astype(jnp.float32)
        blank = jnp.zeros((halo, BLOCK - width), jnp.float32)
        target[:halo, :] = jnp.concatenate([turned, blank], axis=1).astype(jnp.bfloat16)
        target[halo:, :] = jnp.broadcast_to(order, (16, BLOCK)).astype(jnp.bfloat16)


def stage_kernel(count, *refs):
    after, feat = refs[:2]
    sources, targets = refs[2 : 2 + count], refs[2 + count : 2 + 2 * count]
    turned, flat, sems = refs[2 + 2 * count :]
    del after
    copies = start_copies([(feat, flat)] + list(zip(sources, targets)), sems)
    copies[0].wait()
    for i in range(turned.shape[0] // BLOCK):
        part = flat[:, i * BLOCK : (i + 1) * BLOCK].astype(jnp.float32)
        turned[i * BLOCK : (i + 1) * BLOCK, :] = jnp.transpose(part).astype(jnp.bfloat16)
    for copy in copies[1:]:
        copy.wait()


def enter_kernel(halo, feat, left, right, links, weights, total, stats, to_last, to_next, order, low, high, columns):
    rows, width = feat.shape
    blank = jnp.zeros((rows, width), jnp.bfloat16)
    edge = jnp.zeros((halo, width), jnp.bfloat16)
    order[...] = jnp.concatenate([left[halo : halo + 1, :], right[halo : halo + 1, :]], axis=0).astype(jnp.float32)
    before = listed(left[:halo, :width], order[0:1, :], 0)
    after = listed(right[:halo, :width], order[1:2, :], 0)
    low[halo : halo + rows, :] = jnp.concatenate([feat[...], blank], axis=1)
    high[halo : halo + rows, :] = jnp.concatenate([blank, feat[...]], axis=1)
    low[:halo, :] = jnp.concatenate([before, edge], axis=1)
    high[:halo, :] = jnp.concatenate([edge, before], axis=1)
    low[halo + rows :, :] = jnp.concatenate([after, edge], axis=1)
    high[halo + rows :, :] = jnp.concatenate([edge, after], axis=1)
    convolve((low, high), links, weights, total, columns, halo)
    summarize(total, stats, to_last, to_next)


def combined(pairs, count):
    mean = functools.reduce(jnp.add, [pair[0:1, :] for pair in pairs]) / len(pairs)
    spread = functools.reduce(jnp.add, [(pair[0:1, :] - mean) * (pair[0:1, :] - mean) for pair in pairs])
    squares = functools.reduce(jnp.add, [pair[1:2, :] for pair in pairs]) + count * spread
    return mean, squares


def norm_of(pairs, count, gain, shift):
    mean, squares = combined([pair[...] for pair in pairs], count)
    scale = lax.rsqrt(squares / (count * len(pairs)) + EPS) * gain[...]
    offset = shift[...]

    def act(raw):
        normed = (raw - mean) * scale + offset
        return (normed * (1.0 + lax.erf(normed * 0.7071067811865476)) * 0.5).astype(jnp.bfloat16)

    return act


def pooled(act):
    rows = act.shape[0]
    row = lax.broadcasted_iota(jnp.int32, (rows // 4, rows), 0)
    col = lax.broadcasted_iota(jnp.int32, (rows // 4, rows), 1)
    quarter = jnp.where((col >= 4 * row) & (col < 4 * row + 4), 0.25, 0.0).astype(jnp.bfloat16)
    return jnp.dot(quarter, act, preferred_element_type=jnp.float32).astype(jnp.bfloat16)


def layer_kernel(halo, listing, pool, count, parts, *refs):
    raw, left, right, order, gain, shift, links, weights = refs[:8]
    pairs = refs[8 : 8 + parts]
    outs = refs[8 + parts :]
    if pool:
        skip, outs = outs[0], outs[1:]
    total, stats, *edges, source, columns = outs
    act = norm_of(pairs, count, gain, shift)
    rows = total.shape[0]
    fold = pooled if pool else (lambda value: value)
    reach = halo * 4 if pool else halo
    source[:halo, :] = listed(fold(act(left[:reach, :])), order[0:1, :], listing)
    source[halo + rows : rows + 2 * halo, :] = listed(fold(act(right[:reach, :])), order[1:2, :], listing)
    if source.shape[0] > rows + 2 * halo:
        source[rows + 2 * halo :, :] = jnp.zeros((source.shape[0] - rows - 2 * halo, source.shape[1]), jnp.bfloat16)
    step = BLOCK
    out_step = step // 4 if pool else step

    def one(i, carry):
        start = pl.multiple_of(i * step, step)
        value = act(raw[pl.ds(start, step), :])
        if pool:
            skip[pl.ds(start, step), :] = value
        source[pl.ds(pl.multiple_of(i * out_step + halo, 16), out_step), :] = fold(value)
        return carry

    lax.fori_loop(0, raw.shape[0] // step, one, 0, unroll=2)
    convolve((source,), links, weights, total, columns, halo)
    summarize(total, stats, *edges)


def last_kernel(count, parts, *refs):
    raw, gain, shift = refs[:3]
    out = refs[3 + parts]
    out[...] = norm_of(refs[3 : 3 + parts], count, gain, shift)(raw[...])


def call(body, outs, scratch, *args, here=(), flops=0, traffic=0):
    args = [pltpu.with_memory_space_constraint(arg, pltpu.HBM) if i in here else arg for i, arg in enumerate(args)]
    return pl.pallas_call(
        body,
        out_shape=outs,
        in_specs=[HERE if i in here else VM for i in range(len(args))],
        out_specs=[VM] * len(outs) if isinstance(outs, (list, tuple)) else VM,
        scratch_shapes=scratch,
        compiler_params=pltpu.CompilerParams(vmem_limit_bytes=16 * 1024 * 1024),
        cost_estimate=pl.CostEstimate(flops=flops, bytes_accessed=traffic, transcendentals=0) if traffic else None,
    )(*args)


def gather_stats(stats, rows):
    count = lax.axis_size(AXES)
    pairs, held, stride = [stats], rows, 1
    while stride < count:
        if stride > 1:
            mean, squares = combined(pairs, held)
            held = held * len(pairs)
            pairs = [jnp.concatenate([mean, squares], axis=0)]
        radix = min(4, count // stride)
        pairs = pairs + [swapped(pairs[0], stride * i) for i in range(1, radix)]
        stride = stride * radix
    return pairs, held


def exchange(stats, to_last, to_next, rows):
    from_left, from_right = shifted(to_next, 1), shifted(to_last, -1)
    pairs, held = gather_stats(stats, rows)
    return from_left, from_right, pairs, held


def f32(*shape):
    return jax.ShapeDtypeStruct(shape, jnp.float32)


def bf16(*shape):
    return jax.ShapeDtypeStruct(shape, jnp.bfloat16)


def conv_outs(rows, channels, edge):
    return [f32(rows, channels), f32(2, channels)] + [f32(edge, channels)] * (2 if edge else 0)


def round_up(value, unit):
    return -(-value // unit) * unit


def per_device(
    features,
    links_fine,
    sends_fine,
    links_mid,
    sends_mid,
    links_coarse,
    sends_coarse,
    kernel_enter,
    gain_enter,
    shift_enter,
    kernel_fine,
    gain_fine,
    shift_fine,
    kernel_widen,
    gain_widen,
    shift_widen,
    kernel_mid,
    gain_mid,
    shift_mid,
    kernel_deep,
    gain_deep,
    shift_deep,
):
    rows_a, rows_b, rows_c = links_fine.shape[1], links_mid.shape[1], links_coarse.shape[1]
    halo_a, halo_b, halo_c = sends_fine.shape[2], sends_mid.shape[2], sends_coarse.shape[2]
    c_a, c_c = kernel_enter.shape[2], kernel_deep.shape[2]

    inner = (rows_a - halo_a, rows_b - halo_b, rows_c - halo_c)
    width = features.shape[1]
    flat = jnp.transpose(features)
    to_last, to_next = call(
        functools.partial(pack_kernel, inner),
        [bf16(halo_a + 16, BLOCK)] * 2,
        [pltpu.VMEM((width, BLOCK), jnp.bfloat16)] * 2
        + [pltpu.VMEM(sends.shape, jnp.int32) for sends in (sends_fine, sends_mid, sends_coarse)]
        + [pltpu.SemaphoreType.DMA((5,))],
        flat,
        sends_fine,
        sends_mid,
        sends_coarse,
        here=range(4),
    )
    left, right = shifted(to_next, 1), shifted(to_last, -1)
    kernels = (kernel_enter, kernel_fine, kernel_widen, kernel_mid, kernel_deep)
    norms = (gain_enter, shift_enter, gain_fine, shift_fine, gain_widen, shift_widen, gain_mid, shift_mid, gain_deep, shift_deep)
    held = [kernel.reshape(TAPS * kernel.shape[1], kernel.shape[2]) for kernel in kernels]
    held = held + list(norms) + [links_fine, links_mid, links_coarse]
    *held, turned = call(
        functools.partial(stage_kernel, len(held)),
        [jax.ShapeDtypeStruct(value.shape, value.dtype) for value in held] + [bf16(rows_a, width)],
        [pltpu.VMEM(flat.shape, jnp.bfloat16), pltpu.SemaphoreType.DMA((len(held) + 1,))],
        to_next,
        flat,
        *held,
        here=range(1, len(held) + 2),
        traffic=8 * 1024 * 1024,
    )
    weights, norms, links = held[:5], held[5:15], held[15:]
    source_a = pltpu.VMEM((round_up(rows_a + 2 * halo_a, BLOCK), 2 * width), jnp.bfloat16)
    *state, order = call(
        functools.partial(enter_kernel, halo_a),
        conv_outs(rows_a, c_a, halo_a) + [f32(2, BLOCK)],
        [source_a, source_a, pltpu.VMEM((rows_a, 5 * BLOCK), jnp.bfloat16)],
        turned,
        left,
        right,
        links[0],
        weights[0],
    )

    def layer(at, state, level, pool, out_edge):
        total, stats, to_last, to_next = state
        rows, halo, listing, links = level
        kernel, gain, shift = weights[at], norms[2 * at - 2], norms[2 * at - 1]
        raw_rows, channels = total.shape
        from_left, from_right, pairs, held = exchange(stats, to_last, to_next, raw_rows)
        outs = conv_outs(rows, kernel.shape[1], out_edge)
        if pool:
            outs = [bf16(raw_rows, channels)] + outs
        return call(
            functools.partial(layer_kernel, halo, listing, pool, held, len(pairs)),
            outs,
            [
                pltpu.VMEM((max(round_up(rows + 2 * halo, BLOCK), WINDOW), channels), jnp.bfloat16),
                pltpu.VMEM((rows, TAPS * channels), jnp.bfloat16),
            ],
            total,
            from_left,
            from_right,
            order,
            gain.reshape(1, -1),
            shift.reshape(1, -1),
            links,
            kernel,
            *pairs,
        )

    level_a = (rows_a, halo_a, 0, links[0])
    level_b = (rows_b, halo_b, halo_a, links[1])
    level_c = (rows_c, halo_c, halo_a + halo_b, links[2])
    state = layer(1, state, level_a, False, 4 * halo_b)
    skip_fine, *state = layer(2, state, level_b, True, halo_b)
    state = layer(3, state, level_b, False, 4 * halo_c)
    skip_mid, *state = layer(4, state, level_c, True, 0)
    total, stats = state
    pairs, count = gather_stats(stats, rows_c)
    bottleneck = call(
        functools.partial(last_kernel, count, len(pairs)),
        bf16(rows_c, c_c),
        [],
        total,
        norms[8].reshape(1, -1),
        norms[9].reshape(1, -1),
        *pairs,
    )
    return (skip_fine, skip_mid, bottleneck)


def solution(mesh):
    split = P(("groups", "face", "sub"), None)
    links, sends = P(None, AXES), P(AXES, None, None)
    return jax.shard_map(
        per_device,
        mesh=mesh,
        in_specs=(split, links, sends, links, sends, links, sends) + (P(),) * 15,
        out_specs=(split, split, split),
        check_vma=False,
    )
```

```python
import functools

import jax
import jax.numpy as jnp
from jax import lax
from jax.experimental import pallas as pl
from jax.experimental.pallas import tpu as pltpu
from jax.sharding import PartitionSpec as P


AXES = ("face", "sub")
BLOCK = 128
WINDOW = 256
TAPS = 9
EPS = 1e-05
STEP = 512
VM = pl.BlockSpec(memory_space=pltpu.VMEM)
HERE = pl.BlockSpec(memory_space=pltpu.HBM)


def shifted(value, steps):
    count = lax.axis_size(AXES)
    return lax.ppermute(value, AXES, [(source, (source + steps) % count) for source in range(count)])


def swapped(value, mask):
    count = lax.axis_size(AXES)
    return lax.ppermute(value, AXES, [(source, source ^ mask) for source in range(count)])


def hots(near, width):
    place = jnp.where((near >= 0) & (near < width), near, -1).astype(jnp.float32).astype(jnp.bfloat16)
    places = lax.broadcasted_iota(jnp.int32, (near.shape[0], width), 1).astype(jnp.float32).astype(jnp.bfloat16)
    one, zero = jnp.bfloat16(1), jnp.bfloat16(0)
    return [jnp.where(place[:, tap : tap + 1] == places, one, zero) for tap in range(TAPS - 1)]


def listed(rows, order, start):
    halo = rows.shape[0]
    column = jnp.transpose(jnp.broadcast_to(order, (BLOCK, BLOCK)))[start : start + halo, :halo]
    places = lax.broadcasted_iota(jnp.int32, (halo, halo), 1).astype(jnp.float32)
    chosen = jnp.where(column == places, 1.0, 0.0).astype(jnp.bfloat16)
    return jnp.dot(chosen, rows, preferred_element_type=jnp.float32).astype(jnp.bfloat16)


def dot(a, b):
    return jnp.dot(a, b, preferred_element_type=jnp.float32)


def spots(links, block, rows, halo):
    link = links[1:, pl.ds(pl.multiple_of(block * BLOCK, BLOCK), BLOCK)]
    place = jnp.where(link < rows, link + halo, jnp.where(link < rows + halo, link - rows, link))
    return jnp.transpose(place)


def mark(links, halo, marks, far):
    rows = links.shape[1]

    def one(block, outside):
        near = spots(links, block, rows, halo) - block * BLOCK
        hot = hots(near, WINDOW)
        for i, part in enumerate(hot[0::2] + hot[1::2]):
            start = pl.multiple_of((block * (TAPS - 1) + i) * BLOCK, BLOCK)
            marks[pl.ds(start, BLOCK), :] = part
        return jnp.maximum(outside, jnp.where((near < 0) | (near >= WINDOW), 1, 0))

    none = jnp.zeros((BLOCK, TAPS - 1), jnp.int32)
    outside = lax.fori_loop(0, rows // BLOCK, one, none, unroll=min(2, rows // BLOCK))
    far[...] = jnp.broadcast_to(jnp.max(outside, axis=0, keepdims=True), far.shape)


def split(rows):
    return [rows[i * BLOCK : (i + 1) * BLOCK] for i in range(rows.shape[0] // BLOCK)]


def picked(sources, even, odd, start, width):
    if len(sources) == 1:
        window = sources[0][pl.ds(start, width), :]
        first = split(dot(even, window).astype(jnp.bfloat16))
        second = split(dot(odd, window).astype(jnp.bfloat16))
        return [part for pair in zip(first, second) for part in pair]
    high = split(dot(even, sources[1][pl.ds(start, width), :]))
    low = split(dot(odd, sources[0][pl.ds(start, width), :]))
    pieces = [high[0]] + [low[i] + high[i + 1] for i in range(3)] + [low[3]]
    return [piece.astype(jnp.bfloat16) for piece in pieces]


def convolve(sources, links, marks, far, weights, total, columns, halo):
    rows, depth = total.shape[0], weights.shape[0]
    padded, lanes = sources[0].shape
    paired = len(sources) == 2
    half = (TAPS - 1) // 2 * BLOCK

    step = min(rows, STEP)

    def gather(block):
        start = block * BLOCK
        own = sources[0][start + halo : start + halo + BLOCK, :]
        even = marks[2 * block * half : (2 * block + 1) * half, :]
        odd = marks[(2 * block + 1) * half : (2 * block + 2) * half, :]
        pieces = picked(sources, even, odd, start, WINDOW)
        pieces = [pieces[0] + own] + pieces[1:] if paired else [own] + pieces
        for i, piece in enumerate(pieces):
            columns[start : start + BLOCK, i * lanes : (i + 1) * lanes] = piece

    def multiply(part):
        total[part * step : (part + 1) * step, :] = dot(columns[part * step : (part + 1) * step, :depth], weights[...])

    for part in range(rows // step):
        for block in range(part * step // BLOCK, (part + 1) * step // BLOCK):
            gather(block)
        if part:
            multiply(part - 1)
    multiply(rows // step - 1)
    if padded <= WINDOW:
        return

    @pl.when(jnp.max(far[...]) > 0)
    def _():
        def rest(block, carry):
            start = pl.multiple_of(block * BLOCK, BLOCK)

            def chunk(place, inner):
                @pl.when((place < block) | (place > block + 1))
                def _():
                    first = pl.multiple_of(place * BLOCK, BLOCK)
                    hot = hots(spots(links, block, rows, halo) - first, BLOCK)
                    even, odd = jnp.concatenate(hot[0::2], axis=0), jnp.concatenate(hot[1::2], axis=0)
                    pieces = picked(sources, even, odd, first, BLOCK)
                    pieces = pieces if paired else [jnp.zeros_like(pieces[0])] + pieces
                    gathered = jnp.concatenate(pieces, axis=1)[:, :depth]
                    total[pl.ds(start, BLOCK), :] += dot(gathered, weights[...])

                return inner

            return lax.fori_loop(0, padded // BLOCK, chunk, carry)

        lax.fori_loop(0, rows // BLOCK, rest, 0)


def summarize(total, stats, *edges):
    rows, _ = total.shape
    pieces = 8
    size = rows // pieces
    sums = [jnp.sum(total[i * size : (i + 1) * size, :], axis=0, keepdims=True) for i in range(pieces)]
    mean = functools.reduce(jnp.add, sums) / rows
    squares = []
    for i in range(pieces):
        centred = total[i * size : (i + 1) * size, :] - mean
        squares.append(jnp.sum(centred * centred, axis=0, keepdims=True))
    stats[...] = jnp.concatenate([mean, functools.reduce(jnp.add, squares)], axis=0)
    for target, start in zip(edges, (0, rows)):
        edge = target.shape[0]
        target[...] = total[start - edge if start else 0 : start or edge, :]


def start_copies(pairs, sems):
    copies = [pltpu.make_async_copy(source, target, sems.at[i]) for i, (source, target) in enumerate(pairs)]
    for copy in copies:
        copy.start()
    return copies


def pack_kernel(inner, feat, sends_a, sends_b, sends_c, to_last, to_next, first, final, *scratch):
    held, sems = scratch[:3], scratch[3]
    width, rows = feat.shape
    pairs = [(feat.at[:, :BLOCK], first), (feat.at[:, rows - BLOCK :], final)]
    for copy in start_copies(pairs + list(zip((sends_a, sends_b, sends_c), held)), sems):
        copy.wait()
    halo = to_next.shape[0] - 16
    for target, edge, side in ((to_last, first, 0), (to_next, final, 1)):
        turned = jnp.transpose(edge[...].astype(jnp.float32))
        turned = turned[BLOCK - halo :] if side else turned[:halo]
        lists = [sends[0, side : side + 1, :] - before * side for sends, before in zip(held, inner)]
        used = sum(part.shape[1] for part in lists)
        order = jnp.concatenate(lists + [jnp.zeros((1, BLOCK - used), jnp.int32)], axis=1).astype(jnp.float32)
        blank = jnp.zeros((halo, BLOCK - width), jnp.float32)
        target[:halo, :] = jnp.concatenate([turned, blank], axis=1).astype(jnp.bfloat16)
        target[halo:, :] = jnp.broadcast_to(order, (16, BLOCK)).astype(jnp.bfloat16)


def stage_kernel(count, halo, *refs):
    after, feat = refs[:2]
    sources, targets = refs[2 : 2 + count], refs[2 + count : 2 + 2 * count]
    turned, marks, far, flat, sems = refs[2 + 2 * count :]
    del after
    copies = start_copies([(sources[0], targets[0]), (feat, flat)] + list(zip(sources[1:], targets[1:])), sems)
    copies[0].wait()
    mark(targets[0], halo, marks, far)
    copies[1].wait()
    for i in range(turned.shape[0] // BLOCK):
        part = flat[:, i * BLOCK : (i + 1) * BLOCK].astype(jnp.float32)
        turned[i * BLOCK : (i + 1) * BLOCK, :] = jnp.transpose(part).astype(jnp.bfloat16)
    for copy in copies[2:]:
        copy.wait()


def mark_kernel(halos, *refs):
    count = len(halos)
    for i, halo in enumerate(halos):
        mark(refs[i], halo, refs[count + 2 * i], refs[count + 2 * i + 1])


def enter_kernel(halo, feat, left, right, links, marks, far, weights, total, stats, to_last, to_next, order, low, high, columns):
    rows, width = feat.shape
    blank = jnp.zeros((rows, width), jnp.bfloat16)
    edge = jnp.zeros((halo, width), jnp.bfloat16)
    order[...] = jnp.concatenate([left[halo : halo + 1, :], right[halo : halo + 1, :]], axis=0).astype(jnp.float32)
    before = listed(left[:halo, :width], order[0:1, :], 0)
    after = listed(right[:halo, :width], order[1:2, :], 0)
    low[halo : halo + rows, :] = jnp.concatenate([feat[...], blank], axis=1)
    high[halo : halo + rows, :] = jnp.concatenate([blank, feat[...]], axis=1)
    low[:halo, :] = jnp.concatenate([before, edge], axis=1)
    high[:halo, :] = jnp.concatenate([edge, before], axis=1)
    low[halo + rows :, :] = jnp.concatenate([after, edge], axis=1)
    high[halo + rows :, :] = jnp.concatenate([edge, after], axis=1)
    convolve((low, high), links, marks, far, weights, total, columns, halo)
    summarize(total, stats, to_last, to_next)


def combined(pairs, count):
    mean = functools.reduce(jnp.add, [pair[0:1, :] for pair in pairs]) / len(pairs)
    spread = functools.reduce(jnp.add, [(pair[0:1, :] - mean) * (pair[0:1, :] - mean) for pair in pairs])
    squares = functools.reduce(jnp.add, [pair[1:2, :] for pair in pairs]) + count * spread
    return mean, squares


def norm_of(pairs, count, gain, shift):
    mean, squares = combined([pair[...] for pair in pairs], count)
    scale = lax.rsqrt(squares / (count * len(pairs)) + EPS) * gain[...]
    offset = shift[...]

    def act(raw):
        normed = (raw - mean) * scale + offset
        return (normed * (1.0 + lax.erf(normed * 0.7071067811865476)) * 0.5).astype(jnp.bfloat16)

    return act


def pooled(act):
    rows = act.shape[0]
    row = lax.broadcasted_iota(jnp.int32, (rows // 4, rows), 0)
    col = lax.broadcasted_iota(jnp.int32, (rows // 4, rows), 1)
    quarter = jnp.where((col >= 4 * row) & (col < 4 * row + 4), 0.25, 0.0).astype(jnp.bfloat16)
    return jnp.dot(quarter, act, preferred_element_type=jnp.float32).astype(jnp.bfloat16)


def layer_kernel(halo, listing, pool, count, parts, *refs):
    raw, left, right, order, gain, shift, links, marks, far, weights = refs[:10]
    pairs = refs[10 : 10 + parts]
    outs = refs[10 + parts :]
    if pool:
        outer, *outs, skip, sem = outs
    total, stats, *edges, source, columns = outs
    act = norm_of(pairs, count, gain, shift)
    rows = total.shape[0]
    fold = pooled if pool else (lambda value: value)
    reach = halo * 4 if pool else halo
    source[:halo, :] = listed(fold(act(left[:reach, :])), order[0:1, :], listing)
    source[halo + rows : rows + 2 * halo, :] = listed(fold(act(right[:reach, :])), order[1:2, :], listing)
    if source.shape[0] > rows + 2 * halo:
        source[rows + 2 * halo :, :] = jnp.zeros((source.shape[0] - rows - 2 * halo, source.shape[1]), jnp.bfloat16)
    step = BLOCK
    out_step = step // 4 if pool else step

    def one(i, carry):
        start = pl.multiple_of(i * step, step)
        value = act(raw[pl.ds(start, step), :])
        if pool:
            skip[pl.ds(start, step), :] = value
        source[pl.ds(pl.multiple_of(i * out_step + halo, 16), out_step), :] = fold(value)
        return carry

    lax.fori_loop(0, raw.shape[0] // step, one, 0, unroll=2)
    if pool:
        copy = pltpu.make_async_copy(skip, outer, sem)
        copy.start()
    convolve((source,), links, marks, far, weights, total, columns, halo)
    summarize(total, stats, *edges)
    if pool:
        copy.wait()


def last_kernel(count, parts, *refs):
    raw, gain, shift = refs[:3]
    out = refs[3 + parts]
    out[...] = norm_of(refs[3 : 3 + parts], count, gain, shift)(raw[...])


def call(body, outs, scratch, *args, here=(), out_here=(), flops=0, traffic=0):
    args = [pltpu.with_memory_space_constraint(arg, pltpu.HBM) if i in here else arg for i, arg in enumerate(args)]
    return pl.pallas_call(
        body,
        out_shape=outs,
        in_specs=[HERE if i in here else VM for i in range(len(args))],
        out_specs=[HERE if i in out_here else VM for i in range(len(outs))] if isinstance(outs, (list, tuple)) else VM,
        scratch_shapes=scratch,
        compiler_params=pltpu.CompilerParams(vmem_limit_bytes=16 * 1024 * 1024),
        cost_estimate=pl.CostEstimate(flops=flops, bytes_accessed=traffic, transcendentals=0) if traffic else None,
    )(*args)


def gather_stats(stats, rows):
    count = lax.axis_size(AXES)
    pairs, held, stride = [stats], rows, 1
    while stride < count:
        if stride > 1:
            mean, squares = combined(pairs, held)
            held = held * len(pairs)
            pairs = [jnp.concatenate([mean, squares], axis=0)]
        radix = min(4, count // stride)
        pairs = pairs + [swapped(pairs[0], stride * i) for i in range(1, radix)]
        stride = stride * radix
    return pairs, held


def exchange(stats, to_last, to_next, rows):
    from_left, from_right = shifted(to_next, 1), shifted(to_last, -1)
    pairs, held = gather_stats(stats, rows)
    return from_left, from_right, pairs, held


def f32(*shape):
    return jax.ShapeDtypeStruct(shape, jnp.float32)


def bf16(*shape):
    return jax.ShapeDtypeStruct(shape, jnp.bfloat16)


def conv_outs(rows, channels, edge):
    return [f32(rows, channels), f32(2, channels)] + [f32(edge, channels)] * (2 if edge else 0)


def mark_outs(rows):
    return [bf16(rows * (TAPS - 1), WINDOW), jax.ShapeDtypeStruct((8, TAPS - 1), jnp.int32)]


def round_up(value, unit):
    return -(-value // unit) * unit


def per_device(
    features,
    links_fine,
    sends_fine,
    links_mid,
    sends_mid,
    links_coarse,
    sends_coarse,
    kernel_enter,
    gain_enter,
    shift_enter,
    kernel_fine,
    gain_fine,
    shift_fine,
    kernel_widen,
    gain_widen,
    shift_widen,
    kernel_mid,
    gain_mid,
    shift_mid,
    kernel_deep,
    gain_deep,
    shift_deep,
):
    rows_a, rows_b, rows_c = links_fine.shape[1], links_mid.shape[1], links_coarse.shape[1]
    halo_a, halo_b, halo_c = sends_fine.shape[2], sends_mid.shape[2], sends_coarse.shape[2]
    c_a, c_c = kernel_enter.shape[2], kernel_deep.shape[2]

    inner = (rows_a - halo_a, rows_b - halo_b, rows_c - halo_c)
    width = features.shape[1]
    flat = jnp.transpose(features)
    to_last, to_next = call(
        functools.partial(pack_kernel, inner),
        [bf16(halo_a + 16, BLOCK)] * 2,
        [pltpu.VMEM((width, BLOCK), jnp.bfloat16)] * 2
        + [pltpu.VMEM(sends.shape, jnp.int32) for sends in (sends_fine, sends_mid, sends_coarse)]
        + [pltpu.SemaphoreType.DMA((5,))],
        flat,
        sends_fine,
        sends_mid,
        sends_coarse,
        here=range(4),
    )
    left, right = shifted(to_next, 1), shifted(to_last, -1)
    kernels = (kernel_enter, kernel_fine, kernel_widen, kernel_mid, kernel_deep)
    norms = (gain_enter, shift_enter, gain_fine, shift_fine, gain_widen, shift_widen, gain_mid, shift_mid, gain_deep, shift_deep)
    held = [kernel.reshape(TAPS * kernel.shape[1], kernel.shape[2]) for kernel in kernels]
    held = [links_fine, links_mid, links_coarse] + held + list(norms)
    *held, turned, marks_a, far_a = call(
        functools.partial(stage_kernel, len(held), halo_a),
        [jax.ShapeDtypeStruct(value.shape, value.dtype) for value in held]
        + [bf16(rows_a, width)]
        + mark_outs(rows_a),
        [pltpu.VMEM(flat.shape, jnp.bfloat16), pltpu.SemaphoreType.DMA((len(held) + 1,))],
        to_next,
        flat,
        *held,
        here=range(1, len(held) + 2),
        traffic=8 * 1024 * 1024,
    )
    links, weights, norms = held[:3], held[3:8], held[8:]
    marks_b, far_b, marks_c, far_c = call(
        functools.partial(mark_kernel, (halo_b, halo_c)),
        mark_outs(rows_b) + mark_outs(rows_c),
        [],
        links[1],
        links[2],
        traffic=4 * 1024 * 1024,
    )
    source_a = pltpu.VMEM((round_up(rows_a + 2 * halo_a, BLOCK), 2 * width), jnp.bfloat16)
    *state, order = call(
        functools.partial(enter_kernel, halo_a),
        conv_outs(rows_a, c_a, halo_a) + [f32(2, BLOCK)],
        [source_a, source_a, pltpu.VMEM((rows_a, 5 * BLOCK), jnp.bfloat16)],
        turned,
        left,
        right,
        links[0],
        marks_a,
        far_a,
        weights[0],
    )

    def layer(at, state, level, pool, out_edge):
        total, stats, to_last, to_next = state
        rows, halo, listing, links = level
        kernel, gain, shift = weights[at], norms[2 * at - 2], norms[2 * at - 1]
        raw_rows, channels = total.shape
        from_left, from_right, pairs, held = exchange(stats, to_last, to_next, raw_rows)
        outs = conv_outs(rows, kernel.shape[1], out_edge)
        if pool:
            outs = [bf16(raw_rows, channels)] + outs
        return call(
            functools.partial(layer_kernel, halo, listing, pool, held, len(pairs)),
            outs,
            [
                pltpu.VMEM((max(round_up(rows + 2 * halo, BLOCK), WINDOW), channels), jnp.bfloat16),
                pltpu.VMEM((rows, TAPS * channels), jnp.bfloat16),
            ]
            + ([pltpu.VMEM((raw_rows, channels), jnp.bfloat16), pltpu.SemaphoreType.DMA] if pool else []),
            total,
            from_left,
            from_right,
            order,
            gain.reshape(1, -1),
            shift.reshape(1, -1),
            *links,
            kernel,
            *pairs,
            out_here=(0,) if pool else (),
        )

    level_a = (rows_a, halo_a, 0, (links[0], marks_a, far_a))
    level_b = (rows_b, halo_b, halo_a, (links[1], marks_b, far_b))
    level_c = (rows_c, halo_c, halo_a + halo_b, (links[2], marks_c, far_c))
    state = layer(1, state, level_a, False, 4 * halo_b)
    skip_fine, *state = layer(2, state, level_b, True, halo_b)
    state = layer(3, state, level_b, False, 4 * halo_c)
    skip_mid, *state = layer(4, state, level_c, True, 0)
    total, stats = state
    pairs, count = gather_stats(stats, rows_c)
    bottleneck = call(
        functools.partial(last_kernel, count, len(pairs)),
        bf16(rows_c, c_c),
        [],
        total,
        norms[8].reshape(1, -1),
        norms[9].reshape(1, -1),
        *pairs,
    )
    return (skip_fine, skip_mid, bottleneck)


def solution(mesh):
    split = P(("groups", "face", "sub"), None)
    links, sends = P(None, AXES), P(AXES, None, None)
    return jax.shard_map(
        per_device,
        mesh=mesh,
        in_specs=(split, links, sends, links, sends, links, sends) + (P(),) * 15,
        out_specs=(split, split, split),
        check_vma=False,
    )
```

```python
import functools

import jax
import jax.numpy as jnp
from jax import lax
from jax.experimental import pallas as pl
from jax.experimental.pallas import tpu as pltpu
from jax.sharding import PartitionSpec as P


AXES = ("face", "sub")
BLOCK = 128
WINDOW = 256
TAPS = 9
EPS = 1e-05
STEP = 512
VM = pl.BlockSpec(memory_space=pltpu.VMEM)
HERE = pl.BlockSpec(memory_space=pltpu.HBM)


def shifted(value, steps):
    count = lax.axis_size(AXES)
    return lax.ppermute(value, AXES, [(source, (source + steps) % count) for source in range(count)])


def swapped(value, mask):
    count = lax.axis_size(AXES)
    return lax.ppermute(value, AXES, [(source, source ^ mask) for source in range(count)])


def hots(near, width):
    place = jnp.where((near >= 0) & (near < width), near, -1).astype(jnp.float32).astype(jnp.bfloat16)
    places = lax.broadcasted_iota(jnp.int32, (near.shape[0], width), 1).astype(jnp.float32).astype(jnp.bfloat16)
    one, zero = jnp.bfloat16(1), jnp.bfloat16(0)
    return [jnp.where(place[:, tap : tap + 1] == places, one, zero) for tap in range(TAPS - 1)]


def listed(rows, order, start):
    halo = rows.shape[0]
    column = jnp.transpose(jnp.broadcast_to(order, (BLOCK, BLOCK)))[start : start + halo, :halo]
    places = lax.broadcasted_iota(jnp.int32, (halo, halo), 1).astype(jnp.float32)
    chosen = jnp.where(column == places, 1.0, 0.0).astype(jnp.bfloat16)
    return jnp.dot(chosen, rows, preferred_element_type=jnp.float32).astype(jnp.bfloat16)


def dot(a, b):
    return jnp.dot(a, b, preferred_element_type=jnp.float32)


def spots(links, block, rows, halo):
    link = links[1:, pl.ds(pl.multiple_of(block * BLOCK, BLOCK), BLOCK)]
    place = jnp.where(link < rows, link + halo, jnp.where(link < rows + halo, link - rows, link))
    return jnp.transpose(place)


def mark(links, halo, marks, far):
    rows = links.shape[1]

    def one(block, outside):
        near = spots(links, block, rows, halo) - block * BLOCK
        hot = hots(near, WINDOW)
        for i, part in enumerate(hot[0::2] + hot[1::2]):
            start = pl.multiple_of((block * (TAPS - 1) + i) * BLOCK, BLOCK)
            marks[pl.ds(start, BLOCK), :] = part
        return jnp.maximum(outside, jnp.where((near < 0) | (near >= WINDOW), 1, 0))

    none = jnp.zeros((BLOCK, TAPS - 1), jnp.int32)
    outside = lax.fori_loop(0, rows // BLOCK, one, none, unroll=min(4, rows // BLOCK))
    far[...] = jnp.broadcast_to(jnp.max(outside, axis=0, keepdims=True), far.shape)


def split(rows):
    return [rows[i * BLOCK : (i + 1) * BLOCK] for i in range(rows.shape[0] // BLOCK)]


def picked(sources, even, odd, start, width):
    if len(sources) == 1:
        window = sources[0][pl.ds(start, width), :]
        first = split(dot(even, window).astype(jnp.bfloat16))
        second = split(dot(odd, window).astype(jnp.bfloat16))
        return [part for pair in zip(first, second) for part in pair]
    high = split(dot(even, sources[1][pl.ds(start, width), :]))
    low = split(dot(odd, sources[0][pl.ds(start, width), :]))
    pieces = [high[0]] + [low[i] + high[i + 1] for i in range(3)] + [low[3]]
    return [piece.astype(jnp.bfloat16) for piece in pieces]


def convolve(sources, links, marks, far, weights, total, columns, halo):
    rows, depth = total.shape[0], weights.shape[0]
    padded, lanes = sources[0].shape
    paired = len(sources) == 2
    half = (TAPS - 1) // 2 * BLOCK

    step = min(rows, STEP)

    def gather(block):
        start = block * BLOCK
        own = sources[0][start + halo : start + halo + BLOCK, :]
        even = marks[2 * block * half : (2 * block + 1) * half, :]
        odd = marks[(2 * block + 1) * half : (2 * block + 2) * half, :]
        pieces = picked(sources, even, odd, start, WINDOW)
        pieces = [pieces[0] + own] + pieces[1:] if paired else [own] + pieces
        for i, piece in enumerate(pieces):
            columns[start : start + BLOCK, i * lanes : (i + 1) * lanes] = piece

    def multiply(part):
        total[part * step : (part + 1) * step, :] = dot(columns[part * step : (part + 1) * step, :depth], weights[...])

    for part in range(rows // step):
        for block in range(part * step // BLOCK, (part + 1) * step // BLOCK):
            gather(block)
        if part:
            multiply(part - 1)
    multiply(rows // step - 1)
    if padded <= WINDOW:
        return

    @pl.when(jnp.max(far[...]) > 0)
    def _():
        def rest(block, carry):
            start = pl.multiple_of(block * BLOCK, BLOCK)

            def chunk(place, inner):
                @pl.when((place < block) | (place > block + 1))
                def _():
                    first = pl.multiple_of(place * BLOCK, BLOCK)
                    hot = hots(spots(links, block, rows, halo) - first, BLOCK)
                    even, odd = jnp.concatenate(hot[0::2], axis=0), jnp.concatenate(hot[1::2], axis=0)
                    pieces = picked(sources, even, odd, first, BLOCK)
                    pieces = pieces if paired else [jnp.zeros_like(pieces[0])] + pieces
                    gathered = jnp.concatenate(pieces, axis=1)[:, :depth]
                    total[pl.ds(start, BLOCK), :] += dot(gathered, weights[...])

                return inner

            return lax.fori_loop(0, padded // BLOCK, chunk, carry)

        lax.fori_loop(0, rows // BLOCK, rest, 0)


def summarize(total, stats, *edges):
    rows, _ = total.shape
    pieces = 8
    size = rows // pieces
    sums = [jnp.sum(total[i * size : (i + 1) * size, :], axis=0, keepdims=True) for i in range(pieces)]
    mean = functools.reduce(jnp.add, sums) / rows
    squares = []
    for i in range(pieces):
        centred = total[i * size : (i + 1) * size, :] - mean
        squares.append(jnp.sum(centred * centred, axis=0, keepdims=True))
    stats[...] = jnp.concatenate([mean, functools.reduce(jnp.add, squares)], axis=0)
    for target, start in zip(edges, (0, rows)):
        edge = target.shape[0]
        target[...] = total[start - edge if start else 0 : start or edge, :]


def start_copies(pairs, sems):
    copies = [pltpu.make_async_copy(source, target, sems.at[i]) for i, (source, target) in enumerate(pairs)]
    for copy in copies:
        copy.start()
    return copies


def pack_kernel(inner, feat, sends_a, sends_b, sends_c, to_last, to_next, first, final, *scratch):
    held, sems = scratch[:3], scratch[3]
    width, rows = feat.shape
    pairs = [(feat.at[:, :BLOCK], first), (feat.at[:, rows - BLOCK :], final)]
    for copy in start_copies(pairs + list(zip((sends_a, sends_b, sends_c), held)), sems):
        copy.wait()
    halo = to_next.shape[0] - 16
    for target, edge, side in ((to_last, first, 0), (to_next, final, 1)):
        turned = jnp.transpose(edge[...].astype(jnp.float32))
        turned = turned[BLOCK - halo :] if side else turned[:halo]
        lists = [sends[0, side : side + 1, :] - before * side for sends, before in zip(held, inner)]
        used = sum(part.shape[1] for part in lists)
        order = jnp.concatenate(lists + [jnp.zeros((1, BLOCK - used), jnp.int32)], axis=1).astype(jnp.float32)
        blank = jnp.zeros((halo, BLOCK - width), jnp.float32)
        target[:halo, :] = jnp.concatenate([turned, blank], axis=1).astype(jnp.bfloat16)
        target[halo:, :] = jnp.broadcast_to(order, (16, BLOCK)).astype(jnp.bfloat16)


def stage_kernel(count, halo, *refs):
    after, feat = refs[:2]
    sources, targets = refs[2 : 2 + count], refs[2 + count : 2 + 2 * count]
    turned, marks, far, flat, sems = refs[2 + 2 * count :]
    del after
    copies = start_copies([(sources[0], targets[0]), (feat, flat)] + list(zip(sources[1:], targets[1:])), sems)
    copies[0].wait()
    mark(targets[0], halo, marks, far)
    copies[1].wait()
    for i in range(turned.shape[0] // BLOCK):
        part = flat[:, i * BLOCK : (i + 1) * BLOCK].astype(jnp.float32)
        turned[i * BLOCK : (i + 1) * BLOCK, :] = jnp.transpose(part).astype(jnp.bfloat16)
    for copy in copies[2:]:
        copy.wait()


def mark_kernel(halos, *refs):
    count = len(halos)
    for i, halo in enumerate(halos):
        mark(refs[i], halo, refs[count + 2 * i], refs[count + 2 * i + 1])


def enter_kernel(halo, feat, left, right, links, marks, far, weights, total, stats, to_last, to_next, order, low, high, columns):
    rows, width = feat.shape
    blank = jnp.zeros((rows, width), jnp.bfloat16)
    edge = jnp.zeros((halo, width), jnp.bfloat16)
    order[...] = jnp.concatenate([left[halo : halo + 1, :], right[halo : halo + 1, :]], axis=0).astype(jnp.float32)
    before = listed(left[:halo, :width], order[0:1, :], 0)
    after = listed(right[:halo, :width], order[1:2, :], 0)
    low[halo : halo + rows, :] = jnp.concatenate([feat[...], blank], axis=1)
    high[halo : halo + rows, :] = jnp.concatenate([blank, feat[...]], axis=1)
    low[:halo, :] = jnp.concatenate([before, edge], axis=1)
    high[:halo, :] = jnp.concatenate([edge, before], axis=1)
    low[halo + rows :, :] = jnp.concatenate([after, edge], axis=1)
    high[halo + rows :, :] = jnp.concatenate([edge, after], axis=1)
    convolve((low, high), links, marks, far, weights, total, columns, halo)
    summarize(total, stats, to_last, to_next)


def combined(pairs, count):
    mean = functools.reduce(jnp.add, [pair[0:1, :] for pair in pairs]) / len(pairs)
    spread = functools.reduce(jnp.add, [(pair[0:1, :] - mean) * (pair[0:1, :] - mean) for pair in pairs])
    squares = functools.reduce(jnp.add, [pair[1:2, :] for pair in pairs]) + count * spread
    return mean, squares


def norm_of(pairs, count, gain, shift):
    mean, squares = combined([pair[...] for pair in pairs], count)
    scale = lax.rsqrt(squares / (count * len(pairs)) + EPS) * gain[...]
    offset = shift[...]

    def act(raw):
        normed = (raw - mean) * scale + offset
        return (normed * (1.0 + lax.erf(normed * 0.7071067811865476)) * 0.5).astype(jnp.bfloat16)

    return act


def pooled(act):
    rows = act.shape[0]
    row = lax.broadcasted_iota(jnp.int32, (rows // 4, rows), 0)
    col = lax.broadcasted_iota(jnp.int32, (rows // 4, rows), 1)
    quarter = jnp.where((col >= 4 * row) & (col < 4 * row + 4), 0.25, 0.0).astype(jnp.bfloat16)
    return jnp.dot(quarter, act, preferred_element_type=jnp.float32).astype(jnp.bfloat16)


def layer_kernel(halo, listing, pool, count, parts, *refs):
    raw, left, right, order, gain, shift, links, marks, far, weights = refs[:10]
    pairs = refs[10 : 10 + parts]
    outs = refs[10 + parts :]
    if pool:
        outer, *outs, skip, sem = outs
    total, stats, *edges, source, columns = outs
    act = norm_of(pairs, count, gain, shift)
    rows = total.shape[0]
    fold = pooled if pool else (lambda value: value)
    reach = halo * 4 if pool else halo
    source[:halo, :] = listed(fold(act(left[:reach, :])), order[0:1, :], listing)
    source[halo + rows : rows + 2 * halo, :] = listed(fold(act(right[:reach, :])), order[1:2, :], listing)
    if source.shape[0] > rows + 2 * halo:
        source[rows + 2 * halo :, :] = jnp.zeros((source.shape[0] - rows - 2 * halo, source.shape[1]), jnp.bfloat16)
    step = BLOCK
    out_step = step // 4 if pool else step

    def one(i, carry):
        start = pl.multiple_of(i * step, step)
        value = act(raw[pl.ds(start, step), :])
        if pool:
            skip[pl.ds(start, step), :] = value
        source[pl.ds(pl.multiple_of(i * out_step + halo, 16), out_step), :] = fold(value)
        return carry

    lax.fori_loop(0, raw.shape[0] // step, one, 0, unroll=min(8, raw.shape[0] // step))
    if pool:
        copy = pltpu.make_async_copy(skip, outer, sem)
        copy.start()
    convolve((source,), links, marks, far, weights, total, columns, halo)
    summarize(total, stats, *edges)
    if pool:
        copy.wait()


def last_kernel(count, parts, *refs):
    raw, gain, shift = refs[:3]
    out = refs[3 + parts]
    out[...] = norm_of(refs[3 : 3 + parts], count, gain, shift)(raw[...])


def call(body, outs, scratch, *args, here=(), out_here=(), flops=0, traffic=0):
    args = [pltpu.with_memory_space_constraint(arg, pltpu.HBM) if i in here else arg for i, arg in enumerate(args)]
    return pl.pallas_call(
        body,
        out_shape=outs,
        in_specs=[HERE if i in here else VM for i in range(len(args))],
        out_specs=[HERE if i in out_here else VM for i in range(len(outs))] if isinstance(outs, (list, tuple)) else VM,
        scratch_shapes=scratch,
        compiler_params=pltpu.CompilerParams(vmem_limit_bytes=16 * 1024 * 1024),
        cost_estimate=pl.CostEstimate(flops=flops, bytes_accessed=traffic, transcendentals=0) if traffic else None,
    )(*args)


def phases(count):
    steps, stride = [[1]], 2
    while stride < count:
        radix = 2 if ((count // stride).bit_length() - 1) % 2 else 4
        steps.append([stride * i ^ 1 for i in range(1, radix)])
        stride = stride * radix
    return steps


def gather_stats(stats, rows):
    pairs, held = [stats], rows
    steps = phases(lax.axis_size(AXES))
    for at, masks in enumerate(steps):
        if at:
            mean, squares = combined(pairs, held)
            held = held * len(pairs)
            pairs = [jnp.concatenate([mean, squares], axis=0)]
        pairs = pairs + [swapped(pairs[0], mask) for mask in masks]
    return pairs, held


def exchange(stats, to_last, to_next, rows):
    from_left, from_right = shifted(to_next, 1), shifted(to_last, -1)
    pairs, held = gather_stats(stats, rows)
    return from_left, from_right, pairs, held


def f32(*shape):
    return jax.ShapeDtypeStruct(shape, jnp.float32)


def bf16(*shape):
    return jax.ShapeDtypeStruct(shape, jnp.bfloat16)


def conv_outs(rows, channels, edge):
    return [f32(rows, channels), f32(2, channels)] + [f32(edge, channels)] * (2 if edge else 0)


def mark_outs(rows):
    return [bf16(rows * (TAPS - 1), WINDOW), jax.ShapeDtypeStruct((8, TAPS - 1), jnp.int32)]


def round_up(value, unit):
    return -(-value // unit) * unit


def per_device(
    features,
    links_fine,
    sends_fine,
    links_mid,
    sends_mid,
    links_coarse,
    sends_coarse,
    kernel_enter,
    gain_enter,
    shift_enter,
    kernel_fine,
    gain_fine,
    shift_fine,
    kernel_widen,
    gain_widen,
    shift_widen,
    kernel_mid,
    gain_mid,
    shift_mid,
    kernel_deep,
    gain_deep,
    shift_deep,
):
    rows_a, rows_b, rows_c = links_fine.shape[1], links_mid.shape[1], links_coarse.shape[1]
    halo_a, halo_b, halo_c = sends_fine.shape[2], sends_mid.shape[2], sends_coarse.shape[2]
    c_a, c_c = kernel_enter.shape[2], kernel_deep.shape[2]

    inner = (rows_a - halo_a, rows_b - halo_b, rows_c - halo_c)
    width = features.shape[1]
    flat = jnp.transpose(features)
    to_last, to_next = call(
        functools.partial(pack_kernel, inner),
        [bf16(halo_a + 16, BLOCK)] * 2,
        [pltpu.VMEM((width, BLOCK), jnp.bfloat16)] * 2
        + [pltpu.VMEM(sends.shape, jnp.int32) for sends in (sends_fine, sends_mid, sends_coarse)]
        + [pltpu.SemaphoreType.DMA((5,))],
        flat,
        sends_fine,
        sends_mid,
        sends_coarse,
        here=range(4),
    )
    left, right = shifted(to_next, 1), shifted(to_last, -1)
    kernels = (kernel_enter, kernel_fine, kernel_widen, kernel_mid, kernel_deep)
    norms = (gain_enter, shift_enter, gain_fine, shift_fine, gain_widen, shift_widen, gain_mid, shift_mid, gain_deep, shift_deep)
    held = [kernel.reshape(TAPS * kernel.shape[1], kernel.shape[2]) for kernel in kernels]
    held = [links_fine, links_mid, links_coarse] + held + list(norms)
    *held, turned, marks_a, far_a = call(
        functools.partial(stage_kernel, len(held), halo_a),
        [jax.ShapeDtypeStruct(value.shape, value.dtype) for value in held]
        + [bf16(rows_a, width)]
        + mark_outs(rows_a),
        [pltpu.VMEM(flat.shape, jnp.bfloat16), pltpu.SemaphoreType.DMA((len(held) + 1,))],
        to_next,
        flat,
        *held,
        here=range(1, len(held) + 2),
        traffic=8 * 1024 * 1024,
    )
    links, weights, norms = held[:3], held[3:8], held[8:]
    marks_b, far_b, marks_c, far_c = call(
        functools.partial(mark_kernel, (halo_b, halo_c)),
        mark_outs(rows_b) + mark_outs(rows_c),
        [],
        links[1],
        links[2],
        traffic=4 * 1024 * 1024,
    )
    source_a = pltpu.VMEM((round_up(rows_a + 2 * halo_a, BLOCK), 2 * width), jnp.bfloat16)
    *state, order = call(
        functools.partial(enter_kernel, halo_a),
        conv_outs(rows_a, c_a, halo_a) + [f32(2, BLOCK)],
        [source_a, source_a, pltpu.VMEM((rows_a, 5 * BLOCK), jnp.bfloat16)],
        turned,
        left,
        right,
        links[0],
        marks_a,
        far_a,
        weights[0],
    )

    def layer(at, state, level, pool, out_edge):
        total, stats, to_last, to_next = state
        rows, halo, listing, links = level
        kernel, gain, shift = weights[at], norms[2 * at - 2], norms[2 * at - 1]
        raw_rows, channels = total.shape
        from_left, from_right, pairs, held = exchange(stats, to_last, to_next, raw_rows)
        outs = conv_outs(rows, kernel.shape[1], out_edge)
        if pool:
            outs = [bf16(raw_rows, channels)] + outs
        return call(
            functools.partial(layer_kernel, halo, listing, pool, held, len(pairs)),
            outs,
            [
                pltpu.VMEM((max(round_up(rows + 2 * halo, BLOCK), WINDOW), channels), jnp.bfloat16),
                pltpu.VMEM((rows, TAPS * channels), jnp.bfloat16),
            ]
            + ([pltpu.VMEM((raw_rows, channels), jnp.bfloat16), pltpu.SemaphoreType.DMA] if pool else []),
            total,
            from_left,
            from_right,
            order,
            gain.reshape(1, -1),
            shift.reshape(1, -1),
            *links,
            kernel,
            *pairs,
            out_here=(0,) if pool else (),
        )

    level_a = (rows_a, halo_a, 0, (links[0], marks_a, far_a))
    level_b = (rows_b, halo_b, halo_a, (links[1], marks_b, far_b))
    level_c = (rows_c, halo_c, halo_a + halo_b, (links[2], marks_c, far_c))
    state = layer(1, state, level_a, False, 4 * halo_b)
    skip_fine, *state = layer(2, state, level_b, True, halo_b)
    state = layer(3, state, level_b, False, 4 * halo_c)
    skip_mid, *state = layer(4, state, level_c, True, 0)
    total, stats = state
    pairs, count = gather_stats(stats, rows_c)
    bottleneck = call(
        functools.partial(last_kernel, count, len(pairs)),
        bf16(rows_c, c_c),
        [],
        total,
        norms[8].reshape(1, -1),
        norms[9].reshape(1, -1),
        *pairs,
    )
    return (skip_fine, skip_mid, bottleneck)


def solution(mesh):
    split = P(("groups", "face", "sub"), None)
    links, sends = P(None, AXES), P(AXES, None, None)
    return jax.shard_map(
        per_device,
        mesh=mesh,
        in_specs=(split, links, sends, links, sends, links, sends) + (P(),) * 15,
        out_specs=(split, split, split),
        check_vma=False,
    )
```
